32 devices in a mesh: row: 16 (over z, y, core), col: 2 (over x).
Axes of the slice: x: 2, y: 2, z: 4, core: 2. Of those that a mesh axis runs over, the one named last changes fastest.
Arguments:
- depth: float32 [1024, 512], P('row', 'col'), may hold values from 1 to 3
- momentum_x: float32 [1024, 512], P('row', 'col'), may hold values from -1.2 to 1.2
- momentum_y: float32 [1024, 512], P('row', 'col'), may hold values from -1.2 to 1.2
- bathymetry: float32 [1024, 512], P('row', 'col'), may hold values from 0 to 0.5
- boxes: int32 [64, 4], replicated, may hold values from 0 to 512, as said below
Outputs:
- error_field: float32 [3, 512, 256], P(None, 'row', 'col')
- x_signatures: float32 [64, 3, 256], P('row', None, 'col')
- y_signatures: float32 [64, 3, 512], P('col', None, 'row')
The draws below stay inside these ranges and needn't reach their ends.
Inputs may be any that keep to these rules, and one draw needn't show every extreme that they name: `boxes`: each row is (top, bottom, left, right) with 64 <= bottom - top <= 512 and 32 <= right - left <= 256; some box spans all coarse rows and some box spans all coarse columns.
All inputs are finite; a program needn't handle non-finite values.
Results may differ from the reference program's by a relative error of at most 0.0003.
Values sent between devices are 32-bit elements; how exact they have to be, the bound alone decides.
A program may use at most 64 MiB of HBM per device.

```python
import jax
import jax.numpy as jnp
from jax import lax

CY = 64
BOXES = 64
NY = 1024
NX = 512
NYC = 512
NXC = 256


def draw_boxes(key, part):
    keys = jax.random.split(jax.random.fold_in(key, 7), 4)
    tall = jax.random.randint(keys[0], (BOXES,), NYC // 8, NYC + 1)
    broad = jax.random.randint(keys[1], (BOXES,), NXC // 8, NXC + 1)
    tall = tall.at[1].set(NYC)
    broad = broad.at[0].set(NXC)
    top = jax.random.randint(keys[2], (BOXES,), 0, NYC - tall + 1)
    left = jax.random.randint(keys[3], (BOXES,), 0, NXC - broad + 1)
    return jnp.stack([top, top + tall, left, left + broad], axis=1).astype(jnp.int32)


def block_levels(key, shape, cuts, low, high):
    level, own = 1.0, jax.random.fold_in(key, 6)
    for axis_at, shards_of in cuts:
        heights = jnp.exp(jax.random.uniform(jax.random.fold_in(own, axis_at), (shards_of,), jnp.float32, low / len(cuts), high / len(cuts)))
        level = level * jnp.repeat(heights, shape[axis_at] // shards_of).reshape([-1 if axis == axis_at else 1 for axis in range(len(shape))])
    return level


def bell_draw(rng, extent, scale, bound, cuts=(), held_as=jnp.bfloat16):
    values = jax.random.normal(rng, extent, jnp.float32) * scale
    if len(cuts) > 0:
        values = block_levels(rng, extent, cuts, -0.22, 0.18) * values
    return jnp.clip(values, min=-bound, max=bound).astype(held_as)


def setup_inputs(seed: int = 0) -> dict:
    key_list = jax.random.split(jax.random.key(seed), 6)
    return {
        "depth": jnp.clip(1.0 + 2.0 * jax.random.uniform(key_list[0], (NY, NX), jnp.float32) ** block_levels(key_list[0], (NY, NX), ((0, 16), (1, 2)), -0.2, 0.2), 1.0, 3.0),
        "momentum_x": bell_draw(key_list[1], (NY, NX), 0.3, 1.2, ((0, 16), (1, 2)), jnp.float32),
        "momentum_y": bell_draw(key_list[2], (NY, NX), 0.3, 1.2, ((0, 16), (1, 2)), jnp.float32),
        "bathymetry": jnp.clip(0.5 * jax.random.uniform(key_list[3], (NY, NX), jnp.float32) ** block_levels(key_list[3], (NY, NX), ((0, 16), (1, 2)), -0.2, 0.2), 0.0, 0.5),
        "boxes": draw_boxes(jax.random.fold_in(key_list[5], 71), 0),
    }


GRAVITY = 9.81
TIME_STEP = 0.03
ERROR_SCALE = 1.0 / (3.0 * 0.03)

def minmod(left, right):
    return 0.5 * (jnp.sign(left) + jnp.sign(right)) * jnp.minimum(jnp.abs(left), jnp.abs(right))

def roe_flux(h_left, m_left, n_left, h_right, m_right, n_right):
    u_left = m_left / h_left
    u_right = m_right / h_right
    v_left = n_left / h_left
    v_right = n_right / h_right
    root_left = jnp.sqrt(h_left)
    root_right = jnp.sqrt(h_right)
    weight = root_left + root_right
    u_hat = (root_left * u_left + root_right * u_right) / weight
    v_hat = (root_left * v_left + root_right * v_right) / weight
    celerity = jnp.sqrt(GRAVITY * 0.5 * (h_left + h_right))
    d_h = h_right - h_left
    d_m = m_right - m_left
    d_n = n_right - n_left
    wave_one = ((u_hat + celerity) * d_h - d_m) / (2.0 * celerity)
    wave_two = d_n - v_hat * d_h
    wave_three = (d_m - (u_hat - celerity) * d_h) / (2.0 * celerity)
    speed_one = jnp.abs(u_hat - celerity) * wave_one
    speed_two = jnp.abs(u_hat) * wave_two
    speed_three = jnp.abs(u_hat + celerity) * wave_three
    flux_h = 0.5 * (m_left + m_right) - 0.5 * (speed_one + speed_three)
    press_left = m_left * u_left + 0.5 * GRAVITY * h_left * h_left
    press_right = m_right * u_right + 0.5 * GRAVITY * h_right * h_right
    flux_m = 0.5 * (press_left + press_right) - 0.5 * (speed_one * (u_hat - celerity) + speed_three * (u_hat + celerity))
    flux_n = 0.5 * (m_left * v_left + m_right * v_right) - 0.5 * (speed_one * v_hat + speed_two + speed_three * v_hat)
    return (flux_h, flux_m, flux_n)

def face_states(strip, axis):
    count = strip.shape[axis]

    def part(array, low, high):
        return lax.slice_in_dim(array, low, high, axis=axis)
    diffs = part(strip, 1, count) - part(strip, 0, count - 1)
    slope = minmod(part(diffs, 0, count - 2), part(diffs, 1, count - 1))
    left = part(strip, 1, count - 2) + 0.5 * part(slope, 0, count - 3)
    right = part(strip, 2, count - 1) - 0.5 * part(slope, 1, count - 2)
    return (left, right)

def rate(padded, bed, spacing):
    rows = padded.shape[1]
    cols = padded.shape[2]
    left, right = face_states(padded[:, 2:rows - 2, :], 2)
    f_h, f_m, f_n = roe_flux(left[0], left[1], left[2], right[0], right[1], right[2])
    flux_x = jnp.stack([f_h, f_m, f_n])
    div_x = flux_x[:, :, 1:] - flux_x[:, :, :-1]
    left, right = face_states(padded[:, :, 2:cols - 2], 1)
    g_h, g_m, g_n = roe_flux(left[0], left[2], left[1], right[0], right[2], right[1])
    flux_y = jnp.stack([g_h, g_n, g_m])
    div_y = flux_y[:, 1:, :] - flux_y[:, :-1, :]
    water = padded[0, 2:rows - 2, 2:cols - 2]
    slope_x = (bed[2:rows - 2, 3:cols - 1] - bed[2:rows - 2, 1:cols - 3]) * 0.5
    slope_y = (bed[3:rows - 1, 2:cols - 2] - bed[1:rows - 3, 2:cols - 2]) * 0.5
    source = jnp.stack([jnp.zeros_like(water), -GRAVITY * water * slope_x, -GRAVITY * water * slope_y])
    return (source - div_x - div_y) / spacing

def crop(array, width):
    return array[..., width:array.shape[-2] - width, width:array.shape[-1] - width]

def advance_margin(state, bed, step, spacing):
    first = crop(state, 2) + step * rate(state, bed, spacing)
    second = 0.75 * crop(state, 4) + 0.25 * (crop(first, 2) + step * rate(first, crop(bed, 2), spacing))
    return crop(state, 6) / 3.0 + 2.0 * (crop(second, 2) + step * rate(second, crop(bed, 4), spacing)) / 3.0

def restrict(field):
    lead = field.shape[:-2]
    rows, cols = (field.shape[-2], field.shape[-1])
    return field.reshape(lead + (rows // 2, 2, cols // 2, 2)).sum(axis=(-3, -1)) * 0.25

def reference(depth, momentum_x, momentum_y, bathymetry, boxes):
    total_rows = depth.shape[0]
    bands = total_rows // CY

    def one_band(index):
        rows = (index * CY - 12 + jnp.arange(CY + 24, dtype=jnp.int32)) % total_rows
        pieces = [jnp.take(array, rows, axis=0) for array in (depth, momentum_x, momentum_y, bathymetry)]
        wide = jnp.stack(pieces)
        wide = jnp.concatenate([wide[:, :, -12:], wide, wide[:, :, :12]], axis=2)
        state_wide = wide[:3]
        bed_wide = wide[3]
        fine = advance_margin(state_wide, bed_wide, TIME_STEP, 1.0)
        fine = advance_margin(fine, crop(bed_wide, 6), TIME_STEP, 1.0)
        coarse_all = restrict(wide)
        coarse = advance_margin(coarse_all[:3], coarse_all[3], 2.0 * TIME_STEP, 2.0)
        return jnp.abs(restrict(fine) - coarse) * ERROR_SCALE
    errors = lax.map(one_band, jnp.arange(bands, dtype=jnp.int32))
    error_field = jnp.transpose(errors, (1, 0, 2, 3)).reshape(3, total_rows // 2, errors.shape[3])
    row_ids = jnp.arange(error_field.shape[1], dtype=jnp.int32)
    col_ids = jnp.arange(error_field.shape[2], dtype=jnp.int32)
    row_mask = ((boxes[:, 0:1] <= row_ids[None, :]) & (row_ids[None, :] < boxes[:, 1:2])).astype(jnp.float32)
    col_mask = ((boxes[:, 2:3] <= col_ids[None, :]) & (col_ids[None, :] < boxes[:, 3:4])).astype(jnp.float32)
    height = (boxes[:, 1] - boxes[:, 0]).astype(jnp.float32)
    breadth = (boxes[:, 3] - boxes[:, 2]).astype(jnp.float32)
    row_weight = row_mask / height[:, None]
    col_weight = col_mask / breadth[:, None]
    x_signatures = jnp.einsum('br,krc->bkc', row_weight, error_field, precision=lax.Precision.HIGHEST) * col_mask[:, None, :]
    y_signatures = jnp.einsum('krc,bc->bkr', error_field, col_weight, precision=lax.Precision.HIGHEST) * row_mask[:, None, :]
    return (error_field, x_signatures, y_signatures)
```

```python
import functools

import jax
import jax.numpy as jnp
from jax import lax
from jax.experimental import pallas as pl
from jax.experimental.pallas import tpu as pltpu
from jax.sharding import PartitionSpec as P

GRAVITY = 9.81
TIME_STEP = 0.03
ERROR_SCALE = 1.0 / (3.0 * 0.03)
MESH = pl.DeviceIdType.MESH
HIGHEST = lax.Precision.HIGHEST
L = 128
HALO = 16


def whole(i, n):
    return i >> (n.bit_length() - 1) if n & (n - 1) == 0 else i // n


def rest(i, n):
    return i & (n - 1) if n & (n - 1) == 0 else i % n


def lane_ids(shape):
    return lax.broadcasted_iota(jnp.int32, shape, len(shape) - 1)


def from_left(x, rows, tiles, lane):
    y = pltpu.roll(x, 1, axis=1)
    if tiles == 1:
        return y
    z = jnp.concatenate([y[(tiles - 1) * rows :], y[: (tiles - 1) * rows]], axis=0)
    return jnp.where(lane == 0, z, y)


def from_right(x, rows, tiles, lane, by=1):
    y = pltpu.roll(x, L - by, axis=1)
    if tiles == 1:
        return y
    z = jnp.concatenate([y[rows:], y[:rows]], axis=0)
    return jnp.where(lane >= L - by, z, y)


def minmod(p, q):
    return jnp.maximum(jnp.minimum(p, jnp.maximum(q, 0.0)), jnp.minimum(q, 0.0))


def roe_flux(hl, ml, nl, hr, mr, nr):
    rl = lax.rsqrt(hl)
    rr = lax.rsqrt(hr)
    al = ml * rl
    ar = mr * rr
    bl = nl * rl
    br = nr * rr
    w = 1.0 / (hl * rl + hr * rr)
    u = (al + ar) * w
    v = (bl + br) * w
    x = (0.5 * GRAVITY) * (hl + hr)
    rc = lax.rsqrt(x)
    c = x * rc
    dh = hr - hl
    dm = mr - ml
    dn = nr - nl
    up = u + c
    um = u - c
    a1 = (up * dh - dm) * (0.5 * rc)
    a3 = dh - a1
    a2 = dn - v * dh
    k1 = jnp.abs(um) * a1
    k2 = jnp.abs(u) * a2
    k3 = jnp.abs(up) * a3
    k13 = k1 + k3
    fh = (ml + mr) - k13
    fm = (al * al + ar * ar + (0.5 * GRAVITY) * (hl * hl + hr * hr)) - (k1 * um + k3 * up)
    fn = (al * bl + ar * br) - (k13 * v + k2)
    return fh, fm, fn


def stage(base, src, dst, slopes, flux, ca, cb, scale, starts, count, rows, tiles):
    several = rows * len(starts)
    flat = (tiles * several, L)
    lane = lane_ids(flat)

    def body(t, carry):
        firsts = [start + t * rows for start in starts]

        def at(ref, c, shift):
            return jnp.concatenate(
                [ref[c, k, pl.ds(r + shift, rows), :] for k in range(tiles) for r in firsts],
                axis=0,
            )

        def put(ref, c, value):
            i = 0
            for k in range(tiles):
                for r in firsts:
                    ref[c, k, pl.ds(r, rows), :] = value[i : i + rows]
                    i += rows

        here = [at(src, c, 0) for c in range(3)]
        left, right = [], []
        for c in range(3):
            p = at(src, c, 1) - here[c]
            s0 = minmod(here[c] - at(src, c, -1), p)
            s1 = minmod(at(src, c, 2) - at(src, c, 1), p)
            left.append(here[c] + 0.5 * s0)
            right.append(at(src, c, 1) - 0.5 * s1)
        g = roe_flux(left[0], left[2], left[1], right[0], right[2], right[1])
        g = (g[0], g[2], g[1])
        for c in range(3):
            put(flux, c, g[c])
        left, right = [], []
        for c in range(3):
            prev = from_left(here[c], several, tiles, lane)
            next1 = from_right(here[c], several, tiles, lane)
            next2 = from_right(here[c], several, tiles, lane, 2)
            d = next1 - here[c]
            lo, hi = jnp.minimum(d, 0.0), jnp.maximum(d, 0.0)
            left.append(here[c] + 0.5 * jnp.maximum(jnp.minimum(here[c] - prev, hi), lo))
            right.append(next1 - 0.5 * jnp.maximum(jnp.minimum(next2 - next1, hi), lo))
        f = roe_flux(left[0], left[1], left[2], right[0], right[1], right[2])
        for c in range(3):
            change = (from_left(f[c], several, tiles, lane) - f[c]) + (at(flux, c, -1) - g[c])
            if c > 0:
                change = change + here[0] * at(slopes, c - 1, 0)
            if ca == 0.0:
                new = here[c] + scale * change
            else:
                new = ca * at(base, c, 0) + (cb * here[c] + scale * change)
            put(dst, c, new)
        return carry

    if count == 1:
        body(0, 0)
    else:
        lax.fori_loop(0, count, body, 0, unroll=True)


def bed_slopes(state, slopes, first, need, rows, tiles):
    flat = (tiles * rows, L)
    lane = lane_ids(flat)

    def body(t, carry):
        r = first + t * rows
        bed = state[3, :, pl.ds(r, rows), :].reshape(flat)
        dx = from_right(bed, rows, tiles, lane) - from_left(bed, rows, tiles, lane)
        dy = state[3, :, pl.ds(r + 1, rows), :] - state[3, :, pl.ds(r - 1, rows), :]
        slopes[0, :, pl.ds(r, rows), :] = (-GRAVITY * dx).reshape(tiles, rows, L)
        slopes[1, :, pl.ds(r, rows), :] = -GRAVITY * dy
        return carry

    lax.fori_loop(0, -(-need // rows), body, 0, unroll=True)


def plan(state, bufs):
    for n in range(0, len(bufs), 3):
        base = state if n == 0 else bufs[n - 1]
        yield base, base, bufs[n], 0.0, 1.0
        yield base, bufs[n], bufs[n + 1], 0.75, 0.25
        yield base, bufs[n + 1], bufs[n + 2], 1.0 / 3.0, 2.0 / 3.0


def dot(a, b):
    return jnp.dot(a, b, precision=HIGHEST, preferred_element_type=jnp.float32)


def kernel(
    nr, nc, h_ref, mx_ref, my_ref, bed_ref, box_ref, e_ref, x_ref, y_ref,
    state, bufs, slopes, fluxes, packed, staged, ends,
    side, sbufs, sslopes, sflux, cstate, cbufs, cslopes, cfluxes, cside, csbufs, csslopes, csflux,
    xs, xr, ys, yr, box_held, load_sem, hs_sem, hr_sem, xs_sem, xr_sem, ys_sem, yr_sem,
):
    size = h_ref.shape[0]
    half = size // 2
    total = size + 2 * HALO
    row = lax.axis_index("row")
    col = lax.axis_index("col")
    boxes = box_ref.shape[1]
    per_row = boxes // nr
    per_col = boxes // nc
    pad = xs.shape[1]

    loads = []
    for c, ref in enumerate((h_ref, mx_ref, my_ref, bed_ref)):
        for t in range(2):
            loads.append(
                pltpu.make_async_copy(
                    ref.at[:, pl.ds(t * L, L)],
                    state.at[c, t, pl.ds(HALO, size), :],
                    load_sem.at[2 * c + t],
                )
            )
    loads.append(pltpu.make_async_copy(box_ref, box_held, load_sem.at[8]))
    for copy in loads:
        copy.start()

    peers = [(d, 0) for d in range(1, nr)] + [(0, d) for d in range(1, nc)]
    for dr in (1, nr - 1):
        for dc in (1, nc - 1):
            if (dr, dc) not in peers:
                peers.append((dr, dc))

    def device(dr, dc):
        return (lax.rem(row + dr, nr), lax.rem(col + dc, nc))

    barrier = pltpu.get_barrier_semaphore()
    for dr, dc in peers:
        pl.semaphore_signal(barrier, inc=1, device_id=device(dr, dc), device_id_type=MESH)
    for copy in loads:
        copy.wait()
    if nc == 2:
        low = lane_ids((size, L)) < L // 2
        for c in range(4):
            packed[c] = jnp.where(
                low, state[c, 0, pl.ds(HALO, size), :], state[c, 1, pl.ds(HALO, size), :]
            )
    pl.semaphore_wait(barrier, len(peers))

    copies = []

    def send(src, dst, dr, dc):
        i = len(copies)
        copies.append(
            pltpu.make_async_remote_copy(
                src_ref=src,
                dst_ref=dst,
                send_sem=hs_sem.at[i],
                recv_sem=hr_sem.at[i],
                device_id=device(dr, dc),
                device_id_type=MESH,
            )
        )
        copies[-1].start()

    top = pl.ds(0, HALO)
    bottom = pl.ds(HALO + size, HALO)
    first_rows = pl.ds(HALO, HALO)
    last_rows = pl.ds(size, HALO)
    middle = pl.ds(HALO, size)
    if nc == 2:
        send(packed.at[:, pl.ds(0, HALO), :], staged.at[0, :, bottom, :], nr - 1, 1)
        send(packed.at[:, pl.ds(size - HALO, HALO), :], staged.at[0, :, top, :], 1, 1)
    else:
        for t, dc in ((0, nc - 1), (1, 1)):
            send(state.at[:, t, first_rows, :], staged.at[t, :, bottom, :], nr - 1, dc)
            send(state.at[:, t, last_rows, :], staged.at[t, :, top, :], 1, dc)
    send(state.at[:, :, first_rows, :], ends.at[1], nr - 1, 0)
    send(state.at[:, :, last_rows, :], ends.at[0], 1, 0)
    if nc == 2:
        send(packed, staged.at[0, :, middle, :], 0, 1)
    else:
        send(state.at[:, 0, middle, :], staged.at[0, :, middle, :], 0, nc - 1)
        send(state.at[:, 1, middle, :], staged.at[1, :, middle, :], 0, 1)

    box = box_held[...].astype(jnp.float32)

    def turned(pick):
        return lax.dot_general(
            pick.astype(jnp.float32), box, (((1,), (1,)), ((), ())), precision=HIGHEST,
            preferred_element_type=jnp.float32,
        )

    i = lax.broadcasted_iota(jnp.int32, (nr * pad, boxes), 0)
    part = rest(i, pad)
    pick = whole(i, pad) * per_row + rest(part, per_row) == lane_ids((nr * pad, boxes))
    spread = turned(pick & (part < 3 * per_row))
    i = lax.broadcasted_iota(jnp.int32, (nr * pad, 1), 0)
    j = lane_ids((1, 3 * half))
    y = (row * half + rest(j, half)).astype(jnp.float32)
    inside = (
        (whole(rest(i, pad), per_row) == whole(j, half))
        & (spread[:, 0:1] <= y)
        & (y < spread[:, 1:2])
    )
    x_weight = jnp.where(inside, 1.0 / jnp.maximum(spread[:, 1:2] - spread[:, 0:1], 1.0), 0.0)
    box = turned(
        lax.broadcasted_iota(jnp.int32, (boxes, boxes), 0) == lane_ids((boxes, boxes))
    )
    x = (col * L + lane_ids((1, L))).astype(jnp.float32)
    x_keep = (spread[:, 2:3] <= x) & (x < spread[:, 3:4])
    x = (col * L + lane_ids((1, L))).astype(jnp.float32)
    inside = (box[:, 2:3] <= x) & (x < box[:, 3:4])
    y_weight = jnp.where(inside, 1.0 / (box[:, 3:4] - box[:, 2:3]), 0.0)
    y_keep = (box[:, 0:1] <= y) & (y < box[:, 1:2])
    i = lax.broadcasted_iota(jnp.int32, (2 * L, L), 0)
    pairs = jnp.where(whole(i, 2) == lane_ids((2 * L, L)), 0.25, 0.0)
    i = lax.broadcasted_iota(jnp.int32, (L, L), 0)
    edge = jnp.where(whole(i, 2) == rest(lane_ids((L, L)), L // 2), 0.25, 0.0)

    def row_pairs(ref, c, t, first, count):
        return (
            ref[c, t, pl.ds(first, count, stride=2), :]
            + ref[c, t, pl.ds(first + 1, count, stride=2), :]
        )

    own, cown = HALO, HALO // 2
    fine = list(plan(state, [bufs.at[n] for n in range(6)]))
    coarse = list(plan(cstate, [cbufs.at[n] for n in range(3)]))
    for c in range(4):
        both = jnp.concatenate([row_pairs(state, c, t, own, half) for t in range(2)], axis=1)
        cstate[c, 0, pl.ds(cown, half), :] = dot(both, pairs)
    bed_slopes(state, slopes, own, size, 16, 2)
    bed_slopes(cstate, cslopes, cown, half, 16, 1)

    def run(steps, k, slopes, flux, spacing, step, starts, count, rows, tiles):
        base, src, dst, ca, cb = steps[k]
        scale = cb * step / (2.0 * spacing)
        stage(base, src, dst, slopes, flux, ca, cb, scale, starts, count, rows, tiles)

    fine_k = (1.0, TIME_STEP)
    coarse_k = (2.0, 2.0 * TIME_STEP)
    for k in range(3):
        gone = 2 * (k + 1)
        run(coarse, k, cslopes, cfluxes.at[k], *coarse_k, [cown + gone - 1],
            -(-(half + 1 - 2 * gone) // 32), 32, 1)
    for k in range(6):
        gone = 2 * (k + 1)
        run(fine, k, slopes, fluxes.at[k], *fine_k, [own + gone - 1],
            -(-(size + 1 - 2 * gone) // 16), 16, 2)

    for copy in copies:
        copy.wait()
    for c in range(4):
        for t in range(2):
            state[c, t, top, :] = ends[0, c, t]
            state[c, t, bottom, :] = ends[1, c, t]
    lane = lane_ids((total, L))
    every = pl.ds(0, total)
    for c in range(4):
        right = staged[0, c, every, :]
        left = pltpu.roll(staged[staged.shape[0] - 1, c, every, :], 32, axis=1)
        begin = pltpu.roll(state[c, 0, every, :], 32, axis=1)
        side[c, 0, every, :] = jnp.where(
            lane < 16,
            right,
            jnp.where(lane < 32, left, jnp.where(lane < 80, begin, state[c, 1, every, :])),
        )
    for c in range(4):
        outer = []
        for t in range(2):
            outer.append(
                jnp.concatenate(
                    [row_pairs(state, c, t, first, cown) for first in (0, own + size)], axis=0
                )
            )
        outer = dot(jnp.concatenate(outer, axis=1), pairs)
        cstate[c, 0, pl.ds(0, cown), :] = outer[:cown]
        cstate[c, 0, pl.ds(cown + half, cown), :] = outer[cown:]
        cside[c, 0, pl.ds(0, total // 2), :] = dot(row_pairs(side, c, 0, 0, total // 2), edge)
    for first in (own - 11, own + size - 4):
        bed_slopes(state, slopes, first, 16, 16, 2)
    for first in (cown - 5, cown + half - 3):
        bed_slopes(cstate, cslopes, first, 8, 8, 1)
    bed_slopes(side, sslopes, own - 10, size + 20, 16, 1)
    bed_slopes(cside, csslopes, cown - 4, half + 8, 16, 1)
    sides = list(plan(side, [sbufs.at[n] for n in range(6)]))
    csides = list(plan(cside, [csbufs.at[n] for n in range(3)]))
    for k in range(3):
        gone = 2 * (k + 1)
        wide = 6 - gone
        run(coarse, k, cslopes, cfluxes.at[k], *coarse_k,
            [cown - wide - 1, cown + half - gone], 1, 8, 1)
        run(csides, k, csslopes, csflux, *coarse_k, [cown - wide - 1],
            -(-(half + 2 * wide + 1) // 24), 24, 1)
    for k in range(6):
        gone = 2 * (k + 1)
        wide = 12 - gone
        run(fine, k, slopes, fluxes.at[k], *fine_k, [own - wide - 1, own + size - gone], 1, 16, 2)
        run(sides, k, sslopes, sflux, *fine_k, [own - wide - 1],
            -(-(size + 2 * wide + 1) // 48), 48, 1)

    errors = []
    lane = lane_ids((half, L))
    for c in range(3):
        edges = row_pairs(sbufs.at[5], c, 0, own, half)
        both = [row_pairs(bufs.at[5], c, t, own, half) for t in range(2)]
        both = [
            jnp.where(lane < 16, pltpu.roll(edges, L - 32, axis=1), both[0]),
            jnp.where(lane >= L - 16, edges, both[1]),
        ]
        edges = csbufs[2, c, 0, pl.ds(cown, half), :]
        rough = jnp.where(lane >= L - 8, edges, cbufs[2, c, 0, pl.ds(cown, half), :])
        rough = jnp.where(lane < 8, pltpu.roll(edges, L - 16, axis=1), rough)
        errors.append(jnp.abs(dot(jnp.concatenate(both, axis=1), pairs) - rough) * ERROR_SCALE)
        e_ref[c] = errors[c]
    error = jnp.concatenate(errors, axis=0)
    xs[...] = jnp.where(x_keep, dot(x_weight, error), 0.0).reshape(nr, pad, L)
    copies = []
    for d in range(1, nr):
        other = lax.rem(row + d, nr)
        copies.append(
            pltpu.make_async_remote_copy(
                src_ref=xs.at[other],
                dst_ref=xr.at[row],
                send_sem=xs_sem.at[d],
                recv_sem=xr_sem.at[d],
                device_id=(other, col),
                device_id_type=MESH,
            )
        )
        copies[-1].start()
    summed = lax.dot_general(
        y_weight, error, (((1,), (1,)), ((), ())), precision=HIGHEST,
        preferred_element_type=jnp.float32,
    )
    ys[:, pl.ds(0, 3 * half)] = jnp.where(y_keep, summed, 0.0)
    for d in range(1, nc):
        other = lax.rem(col + d, nc)
        copies.append(
            pltpu.make_async_remote_copy(
                src_ref=ys.at[pl.ds(pl.multiple_of(other * per_col, 8), per_col), :],
                dst_ref=yr.at[col],
                send_sem=ys_sem.at[d],
                recv_sem=yr_sem.at[d],
                device_id=(row, other),
                device_id_type=MESH,
            )
        )
        copies[-1].start()
    xr[row] = xs[row]
    yr[col] = ys[pl.ds(pl.multiple_of(col * per_col, 8), per_col), :]
    for copy in copies:
        copy.wait()
    x_sum = xr[0]
    for d in range(1, nr):
        x_sum = x_sum + xr[d]
    for c in range(3):
        x_ref[c] = x_sum[c * per_row : (c + 1) * per_row]
    y_sum = yr[0]
    for d in range(1, nc):
        y_sum = y_sum + yr[d]
    for c in range(3):
        y_ref[c] = y_sum[:, c * half : (c + 1) * half]


def on_device(nr, nc, depth, momentum_x, momentum_y, bathymetry, boxes):
    size = depth.shape[0]
    half = size // 2
    number = boxes.shape[0]
    pad = -(-4 * (number // nr) // 8) * 8
    rows = size + 2 * HALO + 32
    crows = half + HALO + 32
    f32 = jnp.float32
    vmem = pltpu.VMEM
    sems = pltpu.SemaphoreType.DMA
    halo_copies = 5 if nc == 2 else 8
    hbm = pl.BlockSpec(memory_space=pltpu.HBM)
    inside = pl.BlockSpec(memory_space=pltpu.VMEM)
    error, x_sig, y_sig = pl.pallas_call(
        functools.partial(kernel, nr, nc),
        out_shape=(
            jax.ShapeDtypeStruct((3, half, L), f32),
            jax.ShapeDtypeStruct((3, number // nr, L), f32),
            jax.ShapeDtypeStruct((3, number // nc, half), f32),
        ),
        in_specs=[hbm] * 5,
        out_specs=(inside,) * 3,
        scratch_shapes=[
            vmem((4, 2, rows, L), f32),
            vmem((6, 3, 2, rows, L), f32),
            vmem((2, 2, rows, L), f32),
            vmem((6, 3, 2, rows, L), f32),
            vmem((4, size, L), f32),
            vmem((1 if nc == 2 else 2, 4, size + 2 * HALO, L), f32),
            vmem((2, 4, 2, HALO, L), f32),
            vmem((4, 1, rows, L), f32),
            vmem((6, 3, 1, rows, L), f32),
            vmem((2, 1, rows, L), f32),
            vmem((3, 1, rows, L), f32),
            vmem((4, 1, crows, L), f32),
            vmem((3, 3, 1, crows, L), f32),
            vmem((2, 1, crows, L), f32),
            vmem((3, 3, 1, crows, L), f32),
            vmem((4, 1, crows, L), f32),
            vmem((3, 3, 1, crows, L), f32),
            vmem((2, 1, crows, L), f32),
            vmem((3, 1, crows, L), f32),
            vmem((nr, pad, L), f32),
            vmem((nr, pad, L), f32),
            vmem((number, L), f32),
            vmem((nc, number // nc, L), f32),
            vmem((4, number), jnp.int32),
            sems((9,)),
            sems((halo_copies,)),
            sems((halo_copies,)),
            sems((nr,)),
            sems((nr,)),
            sems((nc,)),
            sems((nc,)),
        ],
        compiler_params=pltpu.CompilerParams(
            collective_id=0, has_side_effects=True, vmem_limit_bytes=63 * 1024 * 1024
        ),
    )(depth, momentum_x, momentum_y, bathymetry, boxes.T)
    return error, jnp.transpose(x_sig, (1, 0, 2)), jnp.transpose(y_sig, (1, 0, 2))


def solution(mesh):
    placed = (P("row", "col"), P("row", "col"), P("row", "col"), P("row", "col"), P())
    return jax.shard_map(
        functools.partial(on_device, mesh.shape["row"], mesh.shape["col"]),
        mesh=mesh,
        in_specs=placed,
        out_specs=(P(None, "row", "col"), P("row", None, "col"), P("col", None, "row")),
        check_vma=False,
    )
```

```python
import functools

import jax
import jax.numpy as jnp
from jax import lax
from jax.experimental import pallas as pl
from jax.experimental.pallas import tpu as pltpu
from jax.sharding import PartitionSpec as P

GRAVITY = 9.81
TIME_STEP = 0.03
ERROR_SCALE = 1.0 / (3.0 * 0.03)
SPEED = 0.5 * TIME_STEP
HELD_H = 0.25 * GRAVITY * SPEED * SPEED
HELD_M = HELD_H * SPEED
HELD_B = 4.0 * HELD_H
MESH = pl.DeviceIdType.MESH
HIGHEST = lax.Precision.HIGHEST
L = 128
HALO = 16


def whole(i, n):
    return i >> (n.bit_length() - 1) if n & (n - 1) == 0 else i // n


def rest(i, n):
    return i & (n - 1) if n & (n - 1) == 0 else i % n


def lane_ids(shape):
    return lax.broadcasted_iota(jnp.int32, shape, len(shape) - 1)


def from_left(x, rows, tiles, lane):
    y = pltpu.roll(x, 1, axis=1)
    if tiles == 1:
        return y
    z = jnp.concatenate([y[(tiles - 1) * rows :], y[: (tiles - 1) * rows]], axis=0)
    return jnp.where(lane == 0, z, y)


def from_right(x, rows, tiles, lane, by=1):
    y = pltpu.roll(x, L - by, axis=1)
    if tiles == 1:
        return y
    z = jnp.concatenate([y[rows:], y[:rows]], axis=0)
    return jnp.where(lane >= L - by, z, y)


def minmod(p, q):
    return jnp.maximum(jnp.minimum(p, jnp.maximum(q, 0.0)), jnp.minimum(q, 0.0))


def roe_flux(hl, ml, nl, hr, mr, nr):
    rl = lax.rsqrt(hl)
    rr = lax.rsqrt(hr)
    al = ml * rl
    ar = mr * rr
    bl = nl * rl
    br = nr * rr
    w = 1.0 / (hl * rl + hr * rr)
    u = (al + ar) * w
    v = (bl + br) * w
    x = hl + hr
    rc = lax.rsqrt(x)
    c = x * rc
    up = u + c
    um = u - c
    dh = hr - hl
    a1 = (up * dh - (mr - ml)) * (0.5 * rc)
    a3 = dh - a1
    a2 = (nr - nl) - v * dh
    k1 = jnp.minimum(um, 0.0) * a1
    k2 = jnp.minimum(u, 0.0) * a2
    k3 = jnp.minimum(up, 0.0) * a3
    k13 = k1 + k3
    fh = ml + k13
    fm = (al * al + hl * hl) + (um * k1 + up * k3)
    fn = al * bl + (v * k13 + k2)
    return fh, fm, fn


def stage(k, base, src, dst, inc, kept, slopes, scratch, blocks, tiles):
    several = sum(rows for _, rows in blocks)
    lane = lane_ids((tiles * several, L))
    sd, sa, st = scratch

    def at(ref, c, shift):
        return jnp.concatenate(
            [ref[c, i, pl.ds(r + shift, rows), :] for i in range(tiles) for r, rows in blocks],
            axis=0,
        )

    def put(ref, c, shift, value):
        n = 0
        for i in range(tiles):
            for r, rows in blocks:
                ref[c, i, pl.ds(r + shift, rows), :] = value[n : n + rows]
                n += rows

    here = [at(src, c, 0) for c in range(3)]
    twice = [x + x for x in here]
    left, right = [], []
    for c in range(3):
        d = at(src, c, 1) - here[c]
        put(sd, c, 0, d)
        s = minmod(at(sd, c, -1), d)
        put(sa, c, 0, twice[c] + s)
        left.append(at(sa, c, -1))
        right.append(twice[c] - s)
    g = roe_flux(left[0], left[2], left[1], right[0], right[2], right[1])
    g = (g[0], g[2], g[1])
    left, right = [], []
    for c in range(3):
        d = from_right(here[c], several, tiles, lane) - here[c]
        s = minmod(from_left(d, several, tiles, lane), d)
        left.append(twice[c] + s)
        right.append(from_right(twice[c] - s, several, tiles, lane))
    f = roe_flux(left[0], left[1], left[2], right[0], right[1], right[2])
    for c in range(3):
        part = (from_left(f[c], several, tiles, lane) - f[c]) + g[c]
        if c > 0:
            part = part + here[0] * at(slopes, c - 1, 0)
        put(st, c, 0, part)
        change = at(st, c, -1) - g[c]
        if k == 1:
            change = 0.25 * (at(inc, c, -1) + change)
        if k == 2:
            change = (2.0 / 3.0) * (at(inc, c, -1) + change)
        if k < 2:
            put(kept, c, -1, change)
        put(dst, c, -1, at(base, c, -1) + change)


def bed_slopes(state, slopes, first, need, rows, tiles):
    flat = (tiles * rows, L)
    lane = lane_ids(flat)

    def body(t, carry):
        r = first + t * rows
        bed = state[3, :, pl.ds(r, rows), :].reshape(flat)
        dx = from_left(bed, rows, tiles, lane) - from_right(bed, rows, tiles, lane)
        dy = state[3, :, pl.ds(r - 1, rows), :] - state[3, :, pl.ds(r + 1, rows), :]
        slopes[0, :, pl.ds(r, rows), :] = dx.reshape(tiles, rows, L)
        slopes[1, :, pl.ds(r, rows), :] = dy
        return carry

    lax.fori_loop(0, -(-need // rows), body, 0, unroll=True)


def plan(state, bufs, incs):
    for n in range(0, len(bufs), 3):
        base = state if n == 0 else bufs[n - 1]
        i = n // 3 * 2
        yield 0, base, base, bufs[n], None, incs[i]
        yield 1, base, bufs[n], bufs[n + 1], incs[i], incs[i + 1]
        yield 2, base, bufs[n + 1], bufs[n + 2], incs[i + 1], None


def dot(a, b):
    return jnp.dot(a, b, precision=HIGHEST, preferred_element_type=jnp.float32)


def kernel(
    nr, nc, h_ref, mx_ref, my_ref, bed_ref, box_ref, e_ref, x_ref, y_ref,
    raw, state, bufs, incs, slopes, sds, sas, sts, packed, staged, ends,
    side, sbufs, sincs, sslopes, ssd, ssa, sst, cstate, cbufs, cincs, cslopes, csds, csas, csts,
    xs, xr, ys, yr, box_held, load_sem, hs_sem, hr_sem, xs_sem, xr_sem, ys_sem, yr_sem,
):
    size = h_ref.shape[0]
    half = size // 2
    total = size + 2 * HALO
    row = lax.axis_index("row")
    col = lax.axis_index("col")
    boxes = box_ref.shape[1]
    per_row = boxes // nr
    per_col = boxes // nc

    peers = []
    near = [(dr, dc) for dr in (nr - 1, 1, 0) for dc in (0, 1, nc - 1) if (dr, dc) != (0, 0)]
    for peer in near + [(d, 0) for d in range(1, nr)] + [(0, d) for d in range(1, nc)]:
        if peer not in peers:
            peers.append(peer)

    def device(dr, dc):
        return (lax.rem(row + dr, nr), lax.rem(col + dc, nc))

    barrier = pltpu.get_barrier_semaphore()
    for dr, dc in peers:
        pl.semaphore_signal(barrier, inc=1, device_id=device(dr, dc), device_id_type=MESH)
    loads = []
    for c, ref in enumerate((h_ref, mx_ref, my_ref, bed_ref)):
        for t in range(2):
            loads.append(
                pltpu.make_async_copy(
                    ref.at[:, pl.ds(t * L, L)],
                    raw.at[c, t],
                    load_sem.at[2 * c + t],
                )
            )
    loads.append(pltpu.make_async_copy(box_ref, box_held, load_sem.at[8]))
    for copy in loads:
        copy.start()


    copies = []

    def send(src, dst, dr, dc):
        i = len(copies)
        copies.append(
            pltpu.make_async_remote_copy(
                src_ref=src,
                dst_ref=dst,
                send_sem=hs_sem.at[i],
                recv_sem=hr_sem.at[i],
                device_id=device(dr, dc),
                device_id_type=MESH,
            )
        )
        copies[-1].start()

    top = pl.ds(0, HALO)
    bottom = pl.ds(HALO + size, HALO)
    middle = pl.ds(HALO, size)
    for copy in loads:
        copy.wait()
    held = (HELD_H, HELD_M, HELD_M, HELD_B)
    lane = lane_ids((size, L))
    pack = None
    for c in range(4):
        both = [raw[c, t] * held[c] for t in range(2)]
        for t in range(2):
            state[c, t, pl.ds(HALO, size), :] = both[t]
        edge = jnp.where(
            rest(lane, 32) < 16,
            pltpu.roll(both[0], 32 * c, axis=1) if c else both[0],
            pltpu.roll(both[1], (32 * c + 32) % L, axis=1),
        )
        pack = edge if pack is None else jnp.where(lane < 32 * c, pack, edge)
    packed[...] = pack
    pl.semaphore_wait(barrier, len(peers))
    send(state.at[:, :, pl.ds(size, HALO), :], ends.at[0], 1, 0)
    send(state.at[:, :, pl.ds(HALO, HALO), :], ends.at[1], nr - 1, 0)
    for t, dc in [(0, nc - 1), (1, 1)][: 1 if nc == 2 else 2]:
        send(packed.at[pl.ds(0, HALO), :], staged.at[t, bottom, :], nr - 1, dc)
        send(packed.at[pl.ds(size - HALO, HALO), :], staged.at[t, top, :], 1, dc)
    later = list(copies)
    for t, dc in [(0, nc - 1), (1, 1)][: 1 if nc == 2 else 2]:
        send(packed, staged.at[t, middle, :], 0, dc)
    sooner = copies[len(later) :]

    box = jnp.transpose(box_held[...].astype(jnp.float32))
    first_y, last_y, first_x, last_x = [box[:, i : i + 1] for i in range(4)]
    y = (row * half + rest(lane_ids((1, 3 * half)), half)).astype(jnp.float32)
    x = (col * L + lane_ids((1, L))).astype(jnp.float32)
    y_inside = (first_y <= y) & (y < last_y)
    x_inside = (first_x <= x) & (x < last_x)
    x_weight = jnp.where(y_inside[:, :half], 1.0, 0.0)
    y_weight = jnp.where(x_inside, 1.0, 0.0)
    x_keep = jnp.where(x_inside, 1.0 / (last_y - first_y), 0.0)
    y_keep = jnp.where(y_inside, 1.0 / (last_x - first_x), 0.0)
    i = lax.broadcasted_iota(jnp.int32, (2 * L, L), 0)
    pairs = jnp.where(whole(i, 2) == lane_ids((2 * L, L)), 0.25, 0.0)
    i = lax.broadcasted_iota(jnp.int32, (L, L), 0)
    j = lane_ids((L, L))
    edge = jnp.where((whole(i, 2) == rest(j + 60, L // 2)) & (j >= 56) & (j < 96), 0.25, 0.0)

    def row_pairs(ref, c, t, first, count):
        return (
            ref[c, t, pl.ds(first, count, stride=2), :]
            + ref[c, t, pl.ds(first + 1, count, stride=2), :]
        )

    own, cown = HALO, HALO // 2
    fine = list(plan(state, [bufs.at[n] for n in range(6)], [incs.at[n] for n in range(4)]))
    coarse = list(plan(cstate, [cbufs.at[n] for n in range(3)], [cincs.at[n] for n in range(2)]))
    for c in range(4):
        both = jnp.concatenate([row_pairs(state, c, t, own, half) for t in range(2)], axis=1)
        cstate[c, 0, pl.ds(cown, half), :] = dot(both, pairs)
    bed_slopes(state, slopes, own, size, 16, 2)
    bed_slopes(cstate, cslopes, cown, half, 16, 1)

    def up8(n):
        return -(-n // 8) * 8

    for k in range(3):
        gone = 2 * (k + 1)
        stage(*coarse[k], cslopes, (csds.at[k], csas.at[k], csts.at[k]),
              [(cown + gone - 2, up8(half + 3 - 2 * gone))], 1)
    for k in range(6):
        gone = 2 * (k + 1)
        stage(*fine[k], slopes, (sds.at[k], sas.at[k], sts.at[k]),
              [(own + gone - 2, up8(size + 3 - 2 * gone))], 2)

    def turn(x, by):
        return pltpu.roll(x, by % L, axis=1) if by % L else x

    def fill_side(r, rows):
        at = pl.ds(r, rows)
        lane = lane_ids((rows, L))
        for c in range(4):
            right = turn(staged[0, at, :], -32 * c)
            left = right if nc == 2 else turn(staged[1, at, :], -32 * c)
            begin = turn(state[c, 0, at, :], 32)
            side[c, 0, at, :] = jnp.where(
                lane < 16,
                right,
                jnp.where(lane < 32, left, jnp.where(lane < 80, begin, state[c, 1, at, :])),
            )

    def fill_coarse(c, j, rough):
        at = pl.ds(own + half // 2 + j, rough.shape[0])
        lane = lane_ids(rough.shape)
        side[c, 0, at, :] = jnp.where((lane >= 56) & (lane < 96), rough, side[c, 0, at, :])

    for copy in sooner:
        copy.wait()
    fill_side(own, size)
    for c in range(4):
        fill_coarse(c, 0, dot(row_pairs(side, c, 0, own, half), edge))
    bed_slopes(side, sslopes, own, size, size, 1)
    sides = list(plan(side, [sbufs.at[n] for n in range(6)], [sincs.at[n] for n in range(4)]))
    for k in range(6):
        gone = 2 * (k + 1)
        stage(*sides[k], sslopes, (ssd.at[k], ssa.at[k], sst.at[k]),
              [(own + gone - 2, up8(size + 3 - 2 * gone))], 1)

    for copy in later:
        copy.wait()
    for c in range(4):
        for t in range(2):
            state[c, t, top, :] = ends[0, c, t]
            state[c, t, bottom, :] = ends[1, c, t]
    fill_side(0, HALO)
    fill_side(own + size, HALO)
    for c in range(4):
        outer = []
        for t in range(2):
            outer.append(
                jnp.concatenate(
                    [row_pairs(state, c, t, first, cown) for first in (0, own + size)], axis=0
                )
            )
        outer = dot(jnp.concatenate(outer, axis=1), pairs)
        cstate[c, 0, pl.ds(0, cown), :] = outer[:cown]
        cstate[c, 0, pl.ds(cown + half, cown), :] = outer[cown:]
        outer = jnp.concatenate(
            [row_pairs(side, c, 0, first, cown) for first in (0, own + size)], axis=0
        )
        outer = dot(outer, edge)
        fill_coarse(c, -cown, outer[:cown])
        fill_coarse(c, half, outer[cown:])
    for first in (own - 11, own + size - 4):
        bed_slopes(state, slopes, first, 16, 16, 2)
        bed_slopes(side, sslopes, first, 16, 16, 1)
    for first in (own + half // 2 - 5, own + half // 2 + half - 3):
        bed_slopes(side, sslopes, first, 8, 8, 1)
    for first in (cown - 5, cown + half - 3):
        bed_slopes(cstate, cslopes, first, 8, 8, 1)
    for k in range(6):
        gone = 2 * (k + 1)
        wide = 12 - gone
        blocks = [(own - wide - 3, 16), (own + size - gone + 1, 16)]
        stage(*fine[k], slopes, (sds.at[k], sas.at[k], sts.at[k]), blocks, 2)
        if k < 3:
            cblocks = [(cown - 6 + gone - 3, 16), (cown + half - gone + 1, 8)]
            stage(*coarse[k], cslopes, (csds.at[k], csas.at[k], csts.at[k]), cblocks, 1)
            blocks = blocks + [(r + own + half // 2 - cown, rows) for r, rows in cblocks]
        stage(*sides[k], sslopes, (ssd.at[k], ssa.at[k], sst.at[k]), blocks, 1)

    errors = []
    lane = lane_ids((half, L))
    for c in range(3):
        edges = row_pairs(sbufs.at[5], c, 0, own, half)
        both = [row_pairs(bufs.at[5], c, t, own, half) for t in range(2)]
        both = [
            jnp.where(lane < 12, pltpu.roll(edges, L - 32, axis=1), both[0]),
            jnp.where(lane >= L - 12, edges, both[1]),
        ]
        edges = sbufs[2, c, 0, pl.ds(own + half // 2, half), :]
        rough = cbufs[2, c, 0, pl.ds(cown, half), :]
        rough = jnp.where(lane >= L - 6, pltpu.roll(edges, 60, axis=1), rough)
        rough = jnp.where(lane < 6, pltpu.roll(edges, L - 84, axis=1), rough)
        back = ERROR_SCALE / (HELD_M if c else HELD_H)
        errors.append(jnp.abs(dot(jnp.concatenate(both, axis=1), pairs) - rough) * back)
        e_ref[c] = errors[c]
    error = jnp.concatenate(errors, axis=0)
    for c in range(3):
        sums = dot(x_weight, errors[c]) * x_keep
        for d in range(nr):
            xs[d, pl.ds(c * per_row, per_row), :] = sums[d * per_row : (d + 1) * per_row]
    copies = []
    for d in range(1, nr):
        other = lax.rem(row + d, nr)
        copies.append(
            pltpu.make_async_remote_copy(
                src_ref=xs.at[other],
                dst_ref=xr.at[row],
                send_sem=xs_sem.at[d],
                recv_sem=xr_sem.at[d],
                device_id=(other, col),
                device_id_type=MESH,
            )
        )
        copies[-1].start()
    summed = lax.dot_general(
        y_weight, error, (((1,), (1,)), ((), ())), precision=HIGHEST,
        preferred_element_type=jnp.float32,
    )
    ys[:, pl.ds(0, 3 * half)] = summed * y_keep
    for d in range(1, nc):
        other = lax.rem(col + d, nc)
        copies.append(
            pltpu.make_async_remote_copy(
                src_ref=ys.at[pl.ds(pl.multiple_of(other * per_col, 8), per_col), :],
                dst_ref=yr.at[col],
                send_sem=ys_sem.at[d],
                recv_sem=yr_sem.at[d],
                device_id=(row, other),
                device_id_type=MESH,
            )
        )
        copies[-1].start()
    xr[row] = xs[row]
    yr[col] = ys[pl.ds(pl.multiple_of(col * per_col, 8), per_col), :]
    for copy in copies:
        copy.wait()
    x_sum = xr[0]
    for d in range(1, nr):
        x_sum = x_sum + xr[d]
    for c in range(3):
        x_ref[c] = x_sum[c * per_row : (c + 1) * per_row]
    y_sum = yr[0]
    for d in range(1, nc):
        y_sum = y_sum + yr[d]
    for c in range(3):
        y_ref[c] = y_sum[:, c * half : (c + 1) * half]


def write_out(e, x, y, e_out, x_out, y_out, sems):
    pairs = ((e, e_out), (x, x_out), (y, y_out))
    copies = [pltpu.make_async_copy(a, b, sems.at[i]) for i, (a, b) in enumerate(pairs)]
    for copy in copies:
        copy.start()
    for copy in copies:
        copy.wait()


def on_device(nr, nc, depth, momentum_x, momentum_y, bathymetry, boxes):
    size = depth.shape[0]
    half = size // 2
    number = boxes.shape[0]
    pad = -(-4 * (number // nr) // 8) * 8
    rows = size + 2 * HALO + 32
    crows = half + HALO + 32
    f32 = jnp.float32
    vmem = pltpu.VMEM
    sems = pltpu.SemaphoreType.DMA
    halo_copies = 5 if nc == 2 else 8
    hbm = pl.BlockSpec(memory_space=pltpu.HBM)
    inside = pl.BlockSpec(memory_space=pltpu.VMEM)
    shapes = (
        jax.ShapeDtypeStruct((3, half, L), f32),
        jax.ShapeDtypeStruct((3, number // nr, L), f32),
        jax.ShapeDtypeStruct((3, number // nc, half), f32),
    )
    results = pl.pallas_call(
        functools.partial(kernel, nr, nc),
        out_shape=shapes,
        in_specs=[hbm] * 5,
        out_specs=(inside,) * 3,
        scratch_shapes=[
            vmem((4, 2, size, L), f32),
            vmem((4, 2, rows, L), f32),
            vmem((6, 3, 2, rows, L), f32),
            vmem((4, 3, 2, rows, L), f32),
            vmem((2, 2, rows, L), f32),
            vmem((6, 3, 2, rows, L), f32),
            vmem((6, 3, 2, rows, L), f32),
            vmem((6, 3, 2, rows, L), f32),
            vmem((size, L), f32),
            vmem((1 if nc == 2 else 2, size + 2 * HALO, L), f32),
            vmem((2, 4, 2, HALO, L), f32),
            vmem((4, 1, rows, L), f32),
            vmem((6, 3, 1, rows, L), f32),
            vmem((4, 3, 1, rows, L), f32),
            vmem((2, 1, rows, L), f32),
            vmem((6, 3, 1, rows, L), f32),
            vmem((6, 3, 1, rows, L), f32),
            vmem((6, 3, 1, rows, L), f32),
            vmem((4, 1, crows, L), f32),
            vmem((3, 3, 1, crows, L), f32),
            vmem((2, 3, 1, crows, L), f32),
            vmem((2, 1, crows, L), f32),
            vmem((3, 3, 1, crows, L), f32),
            vmem((3, 3, 1, crows, L), f32),
            vmem((3, 3, 1, crows, L), f32),
            vmem((nr, pad, L), f32),
            vmem((nr, pad, L), f32),
            vmem((number, L), f32),
            vmem((nc, number // nc, L), f32),
            vmem((4, number), jnp.int32),
            sems((9,)),
            sems((halo_copies,)),
            sems((halo_copies,)),
            sems((nr,)),
            sems((nr,)),
            sems((nc,)),
            sems((nc,)),
        ],
        compiler_params=pltpu.CompilerParams(
            collective_id=0, has_side_effects=True, vmem_limit_bytes=63 * 1024 * 1024
        ),
    )(depth, momentum_x, momentum_y, bathymetry, boxes.T)
    error, x_sig, y_sig = pl.pallas_call(
        write_out,
        out_shape=shapes,
        in_specs=[inside] * 3,
        out_specs=(hbm,) * 3,
        scratch_shapes=[sems((3,))],
    )(*results)
    return error, jnp.transpose(x_sig, (1, 0, 2)), jnp.transpose(y_sig, (1, 0, 2))


def solution(mesh):
    placed = (P("row", "col"), P("row", "col"), P("row", "col"), P("row", "col"), P())
    return jax.shard_map(
        functools.partial(on_device, mesh.shape["row"], mesh.shape["col"]),
        mesh=mesh,
        in_specs=placed,
        out_specs=(P(None, "row", "col"), P("row", None, "col"), P("col", None, "row")),
        check_vma=False,
    )
```

```python
import functools

import jax
import jax.numpy as jnp
from jax import lax
from jax.experimental import pallas as pl
from jax.experimental.pallas import tpu as pltpu
from jax.sharding import PartitionSpec as P

GRAVITY = 9.81
TIME_STEP = 0.03
ERROR_SCALE = 1.0 / (3.0 * 0.03)
SPEED = 0.5 * TIME_STEP
HELD_H = 0.25 * GRAVITY * SPEED * SPEED
HELD_M = HELD_H * SPEED
HELD_B = 4.0 * HELD_H
MESH = pl.DeviceIdType.MESH
HIGHEST = lax.Precision.HIGHEST
L = 128
HALO = 16
SHORT = 64


def whole(i, n):
    return i >> (n.bit_length() - 1) if n & (n - 1) == 0 else i // n


def rest(i, n):
    return i & (n - 1) if n & (n - 1) == 0 else i % n


def lane_ids(shape):
    return lax.broadcasted_iota(jnp.int32, shape, len(shape) - 1)


def from_left(x, rows, tiles, lane):
    y = pltpu.roll(x, 1, axis=1)
    if tiles == 1:
        return y
    z = jnp.concatenate([y[(tiles - 1) * rows :], y[: (tiles - 1) * rows]], axis=0)
    return jnp.where(lane == 0, z, y)


def from_right(x, rows, tiles, lane, by=1):
    y = pltpu.roll(x, L - by, axis=1)
    if tiles == 1:
        return y
    z = jnp.concatenate([y[rows:], y[:rows]], axis=0)
    return jnp.where(lane >= L - by, z, y)


def minmod(p, q):
    return jnp.maximum(jnp.minimum(p, jnp.maximum(q, 0.0)), jnp.minimum(q, 0.0))


def roe_flux(hl, ml, nl, hr, mr, nr):
    rl = lax.rsqrt(hl)
    rr = lax.rsqrt(hr)
    al = ml * rl
    ar = mr * rr
    bl = nl * rl
    br = nr * rr
    w = 1.0 / (hl * rl + hr * rr)
    u = (al + ar) * w
    v = (bl + br) * w
    x = hl + hr
    rc = lax.rsqrt(x)
    c = x * rc
    up = u + c
    um = u - c
    dh = hr - hl
    a1 = (up * dh - (mr - ml)) * (0.5 * rc)
    a3 = dh - a1
    a2 = (nr - nl) - v * dh
    k1 = jnp.minimum(um, 0.0) * a1
    k2 = jnp.minimum(u, 0.0) * a2
    k3 = jnp.minimum(up, 0.0) * a3
    k13 = k1 + k3
    fh = ml + k13
    fm = (al * al + hl * hl) + (um * k1 + up * k3)
    fn = al * bl + (v * k13 + k2)
    return fh, fm, fn


def stage(k, base, src, dst, inc, kept, slopes, scratch, blocks, tiles):
    several = sum(rows for _, rows in blocks)
    lane = lane_ids((tiles * several, L))
    sd, sa, st = scratch

    def at(ref, c, shift):
        return jnp.concatenate(
            [ref[c, i, pl.ds(r + shift, rows), :] for i in range(tiles) for r, rows in blocks],
            axis=0,
        )

    def put(ref, c, shift, value):
        n = 0
        for i in range(tiles):
            for r, rows in blocks:
                ref[c, i, pl.ds(r + shift, rows), :] = value[n : n + rows]
                n += rows

    here = [at(src, c, 0) for c in range(3)]
    twice = [x + x for x in here]
    left, right = [], []
    for c in range(3):
        d = at(src, c, 1) - here[c]
        put(sd, c, 0, d)
        s = minmod(at(sd, c, -1), d)
        put(sa, c, 0, twice[c] + s)
        left.append(at(sa, c, -1))
        right.append(twice[c] - s)
    yield
    g = roe_flux(left[0], left[2], left[1], right[0], right[2], right[1])
    g = (g[0], g[2], g[1])
    yield
    left, right = [], []
    for c in range(3):
        next1 = from_right(here[c], several, tiles, lane)
        d = next1 - here[c]
        s = minmod(here[c] - from_left(here[c], several, tiles, lane), d)
        left.append(twice[c] + s)
        if tiles * several > SHORT:
            right.append(from_right(twice[c] - s, several, tiles, lane))
        else:
            next2 = from_right(here[c], several, tiles, lane, 2)
            right.append((next1 + next1) - minmod(d, next2 - next1))
    yield
    f = roe_flux(left[0], left[1], left[2], right[0], right[1], right[2])
    yield
    for c in range(3):
        part = (from_left(f[c], several, tiles, lane) - f[c]) + g[c]
        if c > 0:
            part = part + here[0] * at(slopes, c - 1, 0)
        put(st, c, 0, part)
        change = at(st, c, -1) - g[c]
        if k == 1:
            change = 0.25 * (at(inc, c, -1) + change)
        if k == 2:
            change = (2.0 / 3.0) * (at(inc, c, -1) + change)
        if k < 2:
            put(kept, c, -1, change)
        put(dst, c, -1, at(base, c, -1) + change)


def together(*stages):
    stages = list(stages)
    while stages:
        stages = [one for one in stages if next(one, True) is None]


def bed_slopes(state, slopes, first, need, rows, tiles):
    flat = (tiles * rows, L)
    lane = lane_ids(flat)

    def body(t, carry):
        r = first + t * rows
        bed = state[3, :, pl.ds(r, rows), :].reshape(flat)
        dx = from_left(bed, rows, tiles, lane) - from_right(bed, rows, tiles, lane)
        dy = state[3, :, pl.ds(r - 1, rows), :] - state[3, :, pl.ds(r + 1, rows), :]
        slopes[0, :, pl.ds(r, rows), :] = dx.reshape(tiles, rows, L)
        slopes[1, :, pl.ds(r, rows), :] = dy
        return carry

    lax.fori_loop(0, -(-need // rows), body, 0, unroll=True)


def plan(state, bufs, incs):
    for n in range(0, len(bufs), 3):
        base = state if n == 0 else bufs[n - 1]
        i = n // 3 * 2
        yield 0, base, base, bufs[n], None, incs[i]
        yield 1, base, bufs[n], bufs[n + 1], incs[i], incs[i + 1]
        yield 2, base, bufs[n + 1], bufs[n + 2], incs[i + 1], None


def dot(a, b):
    return jnp.dot(a, b, precision=HIGHEST, preferred_element_type=jnp.float32)


def kernel(
    nr, nc, h_ref, mx_ref, my_ref, bed_ref, box_ref, e_ref, x_ref, y_ref,
    raw, state, bufs, incs, slopes, sds, sas, sts, packed, staged, ends,
    side, sbufs, sincs, sslopes, ssd, ssa, sst, cstate, cbufs, cincs, cslopes, csds, csas, csts,
    xs, xr, ys, yr, box_held, load_sem, hs_sem, hr_sem, xs_sem, xr_sem, ys_sem, yr_sem,
):
    size = h_ref.shape[0]
    half = size // 2
    total = size + 2 * HALO
    row = lax.axis_index("row")
    col = lax.axis_index("col")
    boxes = box_ref.shape[1]
    per_row = boxes // nr
    per_col = boxes // nc

    peers = []
    near = [(dr, dc) for dr in (nr - 1, 1, 0) for dc in (0, 1, nc - 1) if (dr, dc) != (0, 0)]
    for peer in near + [(d, 0) for d in range(1, nr)] + [(0, d) for d in range(1, nc)]:
        if peer not in peers:
            peers.append(peer)

    def device(dr, dc):
        return (lax.rem(row + dr, nr), lax.rem(col + dc, nc))

    barrier = pltpu.get_barrier_semaphore()
    for dr, dc in peers:
        pl.semaphore_signal(barrier, inc=1, device_id=device(dr, dc), device_id_type=MESH)
    loads = []
    for c, ref in enumerate((h_ref, mx_ref, my_ref, bed_ref)):
        for t in range(2):
            loads.append(
                pltpu.make_async_copy(
                    ref.at[:, pl.ds(t * L, L)],
                    raw.at[c, t],
                    load_sem.at[2 * c + t],
                )
            )
    loads.append(pltpu.make_async_copy(box_ref, box_held, load_sem.at[8]))
    for copy in loads:
        copy.start()


    copies = []

    def send(src, dst, dr, dc):
        i = len(copies)
        copies.append(
            pltpu.make_async_remote_copy(
                src_ref=src,
                dst_ref=dst,
                send_sem=hs_sem.at[i],
                recv_sem=hr_sem.at[i],
                device_id=device(dr, dc),
                device_id_type=MESH,
            )
        )
        copies[-1].start()

    top = pl.ds(0, HALO)
    bottom = pl.ds(HALO + size, HALO)
    middle = pl.ds(HALO, size)
    for copy in loads:
        copy.wait()
    held = (HELD_H, HELD_M, HELD_M, HELD_B)
    lane = lane_ids((size, L))
    pack = None
    for c in range(4):
        both = [raw[c, t] * held[c] for t in range(2)]
        for t in range(2):
            state[c, t, pl.ds(HALO, size), :] = both[t]
        edge = jnp.where(
            rest(lane, 32) < 16,
            pltpu.roll(both[0], 32 * c, axis=1) if c else both[0],
            pltpu.roll(both[1], (32 * c + 32) % L, axis=1),
        )
        pack = edge if pack is None else jnp.where(lane < 32 * c, pack, edge)
    packed[...] = pack
    pl.semaphore_wait(barrier, len(peers))
    send(state.at[:, :, pl.ds(size, HALO), :], ends.at[0], 1, 0)
    send(state.at[:, :, pl.ds(HALO, HALO), :], ends.at[1], nr - 1, 0)
    for t, dc in [(0, nc - 1), (1, 1)][: 1 if nc == 2 else 2]:
        send(packed.at[pl.ds(0, HALO), :], staged.at[t, bottom, :], nr - 1, dc)
        send(packed.at[pl.ds(size - HALO, HALO), :], staged.at[t, top, :], 1, dc)
    later = list(copies)
    for t, dc in [(0, nc - 1), (1, 1)][: 1 if nc == 2 else 2]:
        send(packed, staged.at[t, middle, :], 0, dc)
    sooner = copies[len(later) :]

    box = jnp.transpose(box_held[...].astype(jnp.float32))
    first_y, last_y, first_x, last_x = [box[:, i : i + 1] for i in range(4)]
    y = (row * half + rest(lane_ids((1, 3 * half)), half)).astype(jnp.float32)
    x = (col * L + lane_ids((1, L))).astype(jnp.float32)
    y_inside = (first_y <= y) & (y < last_y)
    x_inside = (first_x <= x) & (x < last_x)
    x_weight = jnp.where(y_inside[:, :half], 1.0, 0.0)
    y_weight = jnp.where(x_inside, 1.0, 0.0)
    x_keep = jnp.where(x_inside, 1.0 / (last_y - first_y), 0.0)
    y_keep = jnp.where(y_inside, 1.0 / (last_x - first_x), 0.0)
    i = lax.broadcasted_iota(jnp.int32, (2 * L, L), 0)
    pairs = jnp.where(whole(i, 2) == lane_ids((2 * L, L)), 0.25, 0.0)
    i = lax.broadcasted_iota(jnp.int32, (L, L), 0)
    j = lane_ids((L, L))
    edge = jnp.where((whole(i, 2) == rest(j + 60, L // 2)) & (j >= 56) & (j < 96), 0.25, 0.0)

    def row_pairs(ref, c, t, first, count):
        return (
            ref[c, t, pl.ds(first, count, stride=2), :]
            + ref[c, t, pl.ds(first + 1, count, stride=2), :]
        )

    own, cown = HALO, HALO // 2
    fine = list(plan(state, [bufs.at[n] for n in range(6)], [incs.at[n] for n in range(4)]))
    coarse = list(plan(cstate, [cbufs.at[n] for n in range(3)], [cincs.at[n] for n in range(2)]))
    for c in range(4):
        both = jnp.concatenate([row_pairs(state, c, t, own, half) for t in range(2)], axis=1)
        cstate[c, 0, pl.ds(cown, half), :] = dot(both, pairs)
    bed_slopes(state, slopes, own, size, 16, 2)
    bed_slopes(cstate, cslopes, cown, half, 16, 1)

    def up8(n):
        return -(-n // 8) * 8

    def fine_stage(k, blocks):
        return stage(*fine[k], slopes, (sds.at[k], sas.at[k], sts.at[k]), blocks, 2)

    def coarse_stage(k, blocks):
        return stage(*coarse[k], cslopes, (csds.at[k], csas.at[k], csts.at[k]), blocks, 1)

    for k in range(6):
        gone = 2 * (k + 1)
        both = [fine_stage(k, [(own + gone - 2, up8(size + 3 - 2 * gone))])]
        if k < 3:
            both.append(coarse_stage(k, [(cown + gone - 2, up8(half + 3 - 2 * gone))]))
        together(*both)

    def turn(x, by):
        return pltpu.roll(x, by % L, axis=1) if by % L else x

    def fill_side(r, rows):
        at = pl.ds(r, rows)
        lane = lane_ids((rows, L))
        for c in range(4):
            right = turn(staged[0, at, :], -32 * c)
            left = right if nc == 2 else turn(staged[1, at, :], -32 * c)
            begin = turn(state[c, 0, at, :], 32)
            side[c, 0, at, :] = jnp.where(
                lane < 16,
                right,
                jnp.where(lane < 32, left, jnp.where(lane < 80, begin, state[c, 1, at, :])),
            )

    def fill_coarse(c, j, rough):
        at = pl.ds(own + half // 2 + j, rough.shape[0])
        lane = lane_ids(rough.shape)
        side[c, 0, at, :] = jnp.where((lane >= 56) & (lane < 96), rough, side[c, 0, at, :])

    for copy in sooner:
        copy.wait()
    fill_side(own, size)
    for c in range(4):
        fill_coarse(c, 0, dot(row_pairs(side, c, 0, own, half), edge))
    bed_slopes(side, sslopes, own, size, size, 1)
    sides = list(plan(side, [sbufs.at[n] for n in range(6)], [sincs.at[n] for n in range(4)]))

    def side_stage(k, blocks):
        return stage(*sides[k], sslopes, (ssd.at[k], ssa.at[k], sst.at[k]), blocks, 1)

    for k in range(6):
        gone = 2 * (k + 1)
        together(side_stage(k, [(own + gone - 2, up8(size + 3 - 2 * gone))]))

    for copy in later:
        copy.wait()
    for c in range(4):
        for t in range(2):
            state[c, t, top, :] = ends[0, c, t]
            state[c, t, bottom, :] = ends[1, c, t]
    fill_side(0, HALO)
    fill_side(own + size, HALO)
    for c in range(4):
        outer = []
        for t in range(2):
            outer.append(
                jnp.concatenate(
                    [row_pairs(state, c, t, first, cown) for first in (0, own + size)], axis=0
                )
            )
        outer = dot(jnp.concatenate(outer, axis=1), pairs)
        cstate[c, 0, pl.ds(0, cown), :] = outer[:cown]
        cstate[c, 0, pl.ds(cown + half, cown), :] = outer[cown:]
        outer = jnp.concatenate(
            [row_pairs(side, c, 0, first, cown) for first in (0, own + size)], axis=0
        )
        outer = dot(outer, edge)
        fill_coarse(c, -cown, outer[:cown])
        fill_coarse(c, half, outer[cown:])
    for first in (own - 11, own + size - 4):
        bed_slopes(state, slopes, first, 16, 16, 2)
        bed_slopes(side, sslopes, first, 16, 16, 1)
    for first in (own + half // 2 - 5, own + half // 2 + half - 3):
        bed_slopes(side, sslopes, first, 8, 8, 1)
    for first in (cown - 5, cown + half - 3):
        bed_slopes(cstate, cslopes, first, 8, 8, 1)
    for k in range(6):
        gone = 2 * (k + 1)
        wide = 12 - gone
        blocks = [(own - wide - 3, 16), (own + size - gone + 1, 16)]
        all_three = [fine_stage(k, blocks)]
        if k < 3:
            cblocks = [(cown - 6 + gone - 3, 16), (cown + half - gone + 1, 8)]
            all_three.append(coarse_stage(k, cblocks))
            blocks = blocks + [(r + own + half // 2 - cown, rows) for r, rows in cblocks]
        all_three.append(side_stage(k, blocks))
        together(*all_three)

    errors = []
    lane = lane_ids((half, L))
    for c in range(3):
        edges = row_pairs(sbufs.at[5], c, 0, own, half)
        both = [row_pairs(bufs.at[5], c, t, own, half) for t in range(2)]
        both = [
            jnp.where(lane < 12, pltpu.roll(edges, L - 32, axis=1), both[0]),
            jnp.where(lane >= L - 12, edges, both[1]),
        ]
        edges = sbufs[2, c, 0, pl.ds(own + half // 2, half), :]
        rough = cbufs[2, c, 0, pl.ds(cown, half), :]
        rough = jnp.where(lane >= L - 6, pltpu.roll(edges, 60, axis=1), rough)
        rough = jnp.where(lane < 6, pltpu.roll(edges, L - 84, axis=1), rough)
        back = ERROR_SCALE / (HELD_M if c else HELD_H)
        errors.append(jnp.abs(dot(jnp.concatenate(both, axis=1), pairs) - rough) * back)
        e_ref[c] = errors[c]
    error = jnp.concatenate(errors, axis=0)
    for c in range(3):
        sums = dot(x_weight, errors[c]) * x_keep
        for d in range(nr):
            xs[d, pl.ds(c * per_row, per_row), :] = sums[d * per_row : (d + 1) * per_row]
    copies = []
    for d in range(1, nr):
        other = lax.rem(row + d, nr)
        copies.append(
            pltpu.make_async_remote_copy(
                src_ref=xs.at[other, pl.ds(0, 3 * per_row)],
                dst_ref=xr.at[row, pl.ds(0, 3 * per_row)],
                send_sem=xs_sem.at[d],
                recv_sem=xr_sem.at[d],
                device_id=(other, col),
                device_id_type=MESH,
            )
        )
        copies[-1].start()
    summed = lax.dot_general(
        y_weight, error, (((1,), (1,)), ((), ())), precision=HIGHEST,
        preferred_element_type=jnp.float32,
    )
    ys[:, pl.ds(0, 3 * half)] = summed * y_keep
    for d in range(1, nc):
        other = lax.rem(col + d, nc)
        copies.append(
            pltpu.make_async_remote_copy(
                src_ref=ys.at[pl.ds(pl.multiple_of(other * per_col, 8), per_col), :],
                dst_ref=yr.at[col],
                send_sem=ys_sem.at[d],
                recv_sem=yr_sem.at[d],
                device_id=(row, other),
                device_id_type=MESH,
            )
        )
        copies[-1].start()
    xr[row] = xs[row]
    yr[col] = ys[pl.ds(pl.multiple_of(col * per_col, 8), per_col), :]
    for copy in copies:
        copy.wait()
    x_sum = xr[0]
    for d in range(1, nr):
        x_sum = x_sum + xr[d]
    for c in range(3):
        x_ref[c] = x_sum[c * per_row : (c + 1) * per_row]
    y_sum = yr[0]
    for d in range(1, nc):
        y_sum = y_sum + yr[d]
    for c in range(3):
        y_ref[c] = y_sum[:, c * half : (c + 1) * half]


def write_out(e, x, y, e_out, x_out, y_out, sems):
    pairs = ((e, e_out), (x, x_out), (y, y_out))
    copies = [pltpu.make_async_copy(a, b, sems.at[i]) for i, (a, b) in enumerate(pairs)]
    for copy in copies:
        copy.start()
    for copy in copies:
        copy.wait()


def on_device(nr, nc, depth, momentum_x, momentum_y, bathymetry, boxes):
    size = depth.shape[0]
    half = size // 2
    number = boxes.shape[0]
    pad = -(-4 * (number // nr) // 8) * 8
    rows = size + 2 * HALO + 32
    crows = half + HALO + 32
    f32 = jnp.float32
    vmem = pltpu.VMEM
    sems = pltpu.SemaphoreType.DMA
    halo_copies = 5 if nc == 2 else 8
    hbm = pl.BlockSpec(memory_space=pltpu.HBM)
    inside = pl.BlockSpec(memory_space=pltpu.VMEM)
    shapes = (
        jax.ShapeDtypeStruct((3, half, L), f32),
        jax.ShapeDtypeStruct((3, number // nr, L), f32),
        jax.ShapeDtypeStruct((3, number // nc, half), f32),
    )
    results = pl.pallas_call(
        functools.partial(kernel, nr, nc),
        out_shape=shapes,
        in_specs=[hbm] * 5,
        out_specs=(inside,) * 3,
        scratch_shapes=[
            vmem((4, 2, size, L), f32),
            vmem((4, 2, rows, L), f32),
            vmem((6, 3, 2, rows, L), f32),
            vmem((4, 3, 2, rows, L), f32),
            vmem((2, 2, rows, L), f32),
            vmem((6, 3, 2, rows, L), f32),
            vmem((6, 3, 2, rows, L), f32),
            vmem((6, 3, 2, rows, L), f32),
            vmem((size, L), f32),
            vmem((1 if nc == 2 else 2, size + 2 * HALO, L), f32),
            vmem((2, 4, 2, HALO, L), f32),
            vmem((4, 1, rows, L), f32),
            vmem((6, 3, 1, rows, L), f32),
            vmem((4, 3, 1, rows, L), f32),
            vmem((2, 1, rows, L), f32),
            vmem((6, 3, 1, rows, L), f32),
            vmem((6, 3, 1, rows, L), f32),
            vmem((6, 3, 1, rows, L), f32),
            vmem((4, 1, crows, L), f32),
            vmem((3, 3, 1, crows, L), f32),
            vmem((2, 3, 1, crows, L), f32),
            vmem((2, 1, crows, L), f32),
            vmem((3, 3, 1, crows, L), f32),
            vmem((3, 3, 1, crows, L), f32),
            vmem((3, 3, 1, crows, L), f32),
            vmem((nr, pad, L), f32),
            vmem((nr, pad, L), f32),
            vmem((number, L), f32),
            vmem((nc, number // nc, L), f32),
            vmem((4, number), jnp.int32),
            sems((9,)),
            sems((halo_copies,)),
            sems((halo_copies,)),
            sems((nr,)),
            sems((nr,)),
            sems((nc,)),
            sems((nc,)),
        ],
        compiler_params=pltpu.CompilerParams(
            collective_id=0, has_side_effects=True, vmem_limit_bytes=63 * 1024 * 1024
        ),
    )(depth, momentum_x, momentum_y, bathymetry, boxes.T)
    error, x_sig, y_sig = pl.pallas_call(
        write_out,
        out_shape=shapes,
        in_specs=[inside] * 3,
        out_specs=(hbm,) * 3,
        scratch_shapes=[sems((3,))],
    )(*results)
    return error, jnp.transpose(x_sig, (1, 0, 2)), jnp.transpose(y_sig, (1, 0, 2))


def solution(mesh):
    placed = (P("row", "col"), P("row", "col"), P("row", "col"), P("row", "col"), P())
    return jax.shard_map(
        functools.partial(on_device, mesh.shape["row"], mesh.shape["col"]),
        mesh=mesh,
        in_specs=placed,
        out_specs=(P(None, "row", "col"), P("row", None, "col"), P("col", None, "row")),
        check_vma=False,
    )
```

```python
import functools

import jax
import jax.numpy as jnp
from jax import lax
from jax.experimental import pallas as pl
from jax.experimental.pallas import tpu as pltpu
from jax.sharding import PartitionSpec as P

GRAVITY = 9.81
TIME_STEP = 0.03
ERROR_SCALE = 1.0 / (3.0 * 0.03)
SPEED = 0.5 * TIME_STEP
HELD_H = 0.25 * GRAVITY * SPEED * SPEED
HELD_M = HELD_H * SPEED
HELD_B = 4.0 * HELD_H
MESH = pl.DeviceIdType.MESH
HIGHEST = lax.Precision.HIGHEST
L = 128
HALO = 16
SHORT = 64


def whole(i, n):
    return i >> (n.bit_length() - 1) if n & (n - 1) == 0 else i // n


def rest(i, n):
    return i & (n - 1) if n & (n - 1) == 0 else i % n


def lane_ids(shape):
    return lax.broadcasted_iota(jnp.int32, shape, len(shape) - 1)


def from_left(x, rows, tiles, lane):
    y = pltpu.roll(x, 1, axis=1)
    if tiles == 1:
        return y
    z = jnp.concatenate([y[(tiles - 1) * rows :], y[: (tiles - 1) * rows]], axis=0)
    return jnp.where(lane == 0, z, y)


def from_right(x, rows, tiles, lane, by=1):
    y = pltpu.roll(x, L - by, axis=1)
    if tiles == 1:
        return y
    z = jnp.concatenate([y[rows:], y[:rows]], axis=0)
    return jnp.where(lane >= L - by, z, y)


def minmod(p, q):
    return jnp.maximum(jnp.minimum(p, jnp.maximum(q, 0.0)), jnp.minimum(q, 0.0))


def roe_flux(hl, ml, nl, hr, mr, nr):
    rl = lax.rsqrt(hl)
    rr = lax.rsqrt(hr)
    al = ml * rl
    ar = mr * rr
    bl = nl * rl
    br = nr * rr
    w = 1.0 / (hl * rl + hr * rr)
    u = (al + ar) * w
    v = (bl + br) * w
    x = hl + hr
    rc = lax.rsqrt(x)
    c = x * rc
    up = u + c
    um = u - c
    dh = hr - hl
    a1 = (up * dh - (mr - ml)) * (0.5 * rc)
    a3 = dh - a1
    a2 = (nr - nl) - v * dh
    k1 = jnp.minimum(um, 0.0) * a1
    k2 = jnp.minimum(u, 0.0) * a2
    k3 = jnp.minimum(up, 0.0) * a3
    k13 = k1 + k3
    fh = ml + k13
    fm = (al * al + hl * hl) + (um * k1 + up * k3)
    fn = al * bl + (v * k13 + k2)
    return fh, fm, fn


def stage(k, base, src, dst, inc, kept, slopes, scratch, blocks, tiles):
    several = sum(rows for _, rows in blocks)
    lane = lane_ids((tiles * several, L))
    sd, sa, st = scratch

    def at(ref, c, shift):
        return jnp.concatenate(
            [ref[c, i, pl.ds(r + shift, rows), :] for i in range(tiles) for r, rows in blocks],
            axis=0,
        )

    def put(ref, c, shift, value):
        n = 0
        for i in range(tiles):
            for r, rows in blocks:
                ref[c, i, pl.ds(r + shift, rows), :] = value[n : n + rows]
                n += rows

    here = [at(src, c, 0) for c in range(3)]
    twice = [x + x for x in here]
    left, right = [], []
    for c in range(3):
        d = at(src, c, 1) - here[c]
        put(sd, c, 0, d)
        s = minmod(at(sd, c, -1), d)
        put(sa, c, 0, twice[c] + s)
        left.append(at(sa, c, -1))
        right.append(twice[c] - s)
    yield
    g = roe_flux(left[0], left[2], left[1], right[0], right[2], right[1])
    g = (g[0], g[2], g[1])
    yield
    left, right = [], []
    for c in range(3):
        next1 = from_right(here[c], several, tiles, lane)
        d = next1 - here[c]
        s = minmod(here[c] - from_left(here[c], several, tiles, lane), d)
        left.append(twice[c] + s)
        if tiles * several > SHORT:
            right.append(from_right(twice[c] - s, several, tiles, lane))
        else:
            next2 = from_right(here[c], several, tiles, lane, 2)
            right.append((next1 + next1) - minmod(d, next2 - next1))
    yield
    f = roe_flux(left[0], left[1], left[2], right[0], right[1], right[2])
    yield
    for c in range(3):
        part = (from_left(f[c], several, tiles, lane) - f[c]) + g[c]
        if c > 0:
            part = part + here[0] * at(slopes, c - 1, 0)
        put(st, c, 0, part)
        change = at(st, c, -1) - g[c]
        if k == 1:
            change = 0.25 * (at(inc, c, -1) + change)
        if k == 2:
            change = (2.0 / 3.0) * (at(inc, c, -1) + change)
        if k < 2:
            put(kept, c, -1, change)
        put(dst, c, -1, at(base, c, -1) + change)


def together(*stages):
    stages = list(stages)
    while stages:
        stages = [one for one in stages if next(one, True) is None]


def bed_slopes(state, slopes, first, need, rows, tiles):
    flat = (tiles * rows, L)
    lane = lane_ids(flat)

    def body(t, carry):
        r = first + t * rows
        bed = state[3, :, pl.ds(r, rows), :].reshape(flat)
        dx = from_left(bed, rows, tiles, lane) - from_right(bed, rows, tiles, lane)
        dy = state[3, :, pl.ds(r - 1, rows), :] - state[3, :, pl.ds(r + 1, rows), :]
        slopes[0, :, pl.ds(r, rows), :] = dx.reshape(tiles, rows, L)
        slopes[1, :, pl.ds(r, rows), :] = dy
        return carry

    lax.fori_loop(0, -(-need // rows), body, 0, unroll=True)


def plan(state, bufs, incs):
    for n in range(0, len(bufs), 3):
        base = state if n == 0 else bufs[n - 1]
        i = n // 3 * 2
        yield 0, base, base, bufs[n], None, incs[i]
        yield 1, base, bufs[n], bufs[n + 1], incs[i], incs[i + 1]
        yield 2, base, bufs[n + 1], bufs[n + 2], incs[i + 1], None


def dot(a, b):
    return jnp.dot(a, b, precision=HIGHEST, preferred_element_type=jnp.float32)


def kernel(
    nr, nc, h_ref, mx_ref, my_ref, bed_ref, box_ref, e_ref, x_ref, y_ref,
    raw, state, bufs, incs, slopes, sds, sas, sts, packed, staged, ends,
    side, sbufs, sincs, sslopes, ssd, ssa, sst, cstate, cbufs, cincs, cslopes, csds, csas, csts,
    xs, xr, ys, yr, box_held, e_held, load_sem, hs_sem, hr_sem, xs_sem, xr_sem, ys_sem, yr_sem,
):
    size = h_ref.shape[0]
    half = size // 2
    total = size + 2 * HALO
    row = lax.axis_index("row")
    col = lax.axis_index("col")
    boxes = box_ref.shape[1]
    per_row = boxes // nr
    per_col = boxes // nc

    peers = []
    near = [(dr, dc) for dr in (nr - 1, 1, 0) for dc in (0, 1, nc - 1) if (dr, dc) != (0, 0)]
    for peer in near + [(d, 0) for d in range(1, nr)] + [(0, d) for d in range(1, nc)]:
        if peer not in peers:
            peers.append(peer)

    def device(dr, dc):
        return (lax.rem(row + dr, nr), lax.rem(col + dc, nc))

    barrier = pltpu.get_barrier_semaphore()
    for dr, dc in peers:
        pl.semaphore_signal(barrier, inc=1, device_id=device(dr, dc), device_id_type=MESH)
    loads = []
    for c, ref in enumerate((h_ref, mx_ref, my_ref, bed_ref)):
        for t in range(2):
            loads.append(
                pltpu.make_async_copy(
                    ref.at[:, pl.ds(t * L, L)],
                    raw.at[c, t],
                    load_sem.at[2 * c + t],
                )
            )
    loads.append(pltpu.make_async_copy(box_ref, box_held, load_sem.at[8]))
    for copy in loads:
        copy.start()


    copies = []

    def send(src, dst, dr, dc):
        i = len(copies)
        copies.append(
            pltpu.make_async_remote_copy(
                src_ref=src,
                dst_ref=dst,
                send_sem=hs_sem.at[i],
                recv_sem=hr_sem.at[i],
                device_id=device(dr, dc),
                device_id_type=MESH,
            )
        )
        copies[-1].start()

    top = pl.ds(0, HALO)
    bottom = pl.ds(HALO + size, HALO)
    middle = pl.ds(HALO, size)
    for copy in loads:
        copy.wait()
    held = (HELD_H, HELD_M, HELD_M, HELD_B)
    lane = lane_ids((size, L))
    pack = None
    for c in range(4):
        both = [raw[c, t] * held[c] for t in range(2)]
        for t in range(2):
            state[c, t, pl.ds(HALO, size), :] = both[t]
        edge = jnp.where(
            rest(lane, 32) < 16,
            pltpu.roll(both[0], 32 * c, axis=1) if c else both[0],
            pltpu.roll(both[1], (32 * c + 32) % L, axis=1),
        )
        pack = edge if pack is None else jnp.where(lane < 32 * c, pack, edge)
    packed[...] = pack
    pl.semaphore_wait(barrier, len(peers))
    send(state.at[:, :, pl.ds(size, HALO), :], ends.at[0], 1, 0)
    send(state.at[:, :, pl.ds(HALO, HALO), :], ends.at[1], nr - 1, 0)
    for t, dc in [(0, nc - 1), (1, 1)][: 1 if nc == 2 else 2]:
        send(packed.at[pl.ds(0, HALO), :], staged.at[t, bottom, :], nr - 1, dc)
        send(packed.at[pl.ds(size - HALO, HALO), :], staged.at[t, top, :], 1, dc)
    later = list(copies)
    for t, dc in [(0, nc - 1), (1, 1)][: 1 if nc == 2 else 2]:
        send(packed, staged.at[t, middle, :], 0, dc)
    sooner = copies[len(later) :]

    box = jnp.transpose(box_held[...].astype(jnp.float32))
    first_y, last_y, first_x, last_x = [box[:, i : i + 1] for i in range(4)]
    y = (row * half + rest(lane_ids((1, 3 * half)), half)).astype(jnp.float32)
    x = (col * L + lane_ids((1, L))).astype(jnp.float32)
    y_inside = (first_y <= y) & (y < last_y)
    x_inside = (first_x <= x) & (x < last_x)
    x_weight = jnp.where(y_inside[:, :half], 1.0, 0.0)
    y_weight = jnp.where(x_inside, 1.0, 0.0)
    x_keep = jnp.where(x_inside, 1.0 / (last_y - first_y), 0.0)
    y_keep = jnp.where(y_inside, 1.0 / (last_x - first_x), 0.0)
    i = lax.broadcasted_iota(jnp.int32, (2 * L, L), 0)
    pairs = jnp.where(whole(i, 2) == lane_ids((2 * L, L)), 0.25, 0.0)
    i = lax.broadcasted_iota(jnp.int32, (L, L), 0)
    j = lane_ids((L, L))
    edge = jnp.where((whole(i, 2) == rest(j + 60, L // 2)) & (j >= 56) & (j < 96), 0.25, 0.0)

    def row_pairs(ref, c, t, first, count):
        return (
            ref[c, t, pl.ds(first, count, stride=2), :]
            + ref[c, t, pl.ds(first + 1, count, stride=2), :]
        )

    own, cown = HALO, HALO // 2
    fine = list(plan(state, [bufs.at[n] for n in range(6)], [incs.at[n] for n in range(4)]))
    coarse = list(plan(cstate, [cbufs.at[n] for n in range(3)], [cincs.at[n] for n in range(2)]))
    for c in range(4):
        both = jnp.concatenate([row_pairs(state, c, t, own, half) for t in range(2)], axis=1)
        cstate[c, 0, pl.ds(cown, half), :] = dot(both, pairs)
    bed_slopes(state, slopes, own, size, 16, 2)
    bed_slopes(cstate, cslopes, cown, half, 16, 1)

    def up8(n):
        return -(-n // 8) * 8

    def fine_stage(k, blocks):
        return stage(*fine[k], slopes, (sds.at[k], sas.at[k], sts.at[k]), blocks, 2)

    def coarse_stage(k, blocks):
        return stage(*coarse[k], cslopes, (csds.at[k], csas.at[k], csts.at[k]), blocks, 1)

    for k in range(6):
        gone = 2 * (k + 1)
        both = [fine_stage(k, [(own + gone - 2, up8(size + 3 - 2 * gone))])]
        if k < 3:
            both.append(coarse_stage(k, [(cown + gone - 2, up8(half + 3 - 2 * gone))]))
        together(*both)

    def turn(x, by):
        return pltpu.roll(x, by % L, axis=1) if by % L else x

    def fill_side(r, rows):
        at = pl.ds(r, rows)
        lane = lane_ids((rows, L))
        for c in range(4):
            right = turn(staged[0, at, :], -32 * c)
            left = right if nc == 2 else turn(staged[1, at, :], -32 * c)
            begin = turn(state[c, 0, at, :], 32)
            side[c, 0, at, :] = jnp.where(
                lane < 16,
                right,
                jnp.where(lane < 32, left, jnp.where(lane < 80, begin, state[c, 1, at, :])),
            )

    def fill_coarse(c, j, rough):
        at = pl.ds(own + half // 2 + j, rough.shape[0])
        lane = lane_ids(rough.shape)
        side[c, 0, at, :] = jnp.where((lane >= 56) & (lane < 96), rough, side[c, 0, at, :])

    for copy in sooner:
        copy.wait()
    fill_side(own, size)
    for c in range(4):
        fill_coarse(c, 0, dot(row_pairs(side, c, 0, own, half), edge))
    bed_slopes(side, sslopes, own, size, size, 1)
    sides = list(plan(side, [sbufs.at[n] for n in range(6)], [sincs.at[n] for n in range(4)]))

    def side_stage(k, blocks):
        return stage(*sides[k], sslopes, (ssd.at[k], ssa.at[k], sst.at[k]), blocks, 1)

    for k in range(6):
        gone = 2 * (k + 1)
        together(side_stage(k, [(own + gone - 2, up8(size + 3 - 2 * gone))]))

    for copy in later:
        copy.wait()
    for c in range(4):
        for t in range(2):
            state[c, t, top, :] = ends[0, c, t]
            state[c, t, bottom, :] = ends[1, c, t]
    fill_side(0, HALO)
    fill_side(own + size, HALO)
    for c in range(4):
        outer = []
        for t in range(2):
            outer.append(
                jnp.concatenate(
                    [row_pairs(state, c, t, first, cown) for first in (0, own + size)], axis=0
                )
            )
        outer = dot(jnp.concatenate(outer, axis=1), pairs)
        cstate[c, 0, pl.ds(0, cown), :] = outer[:cown]
        cstate[c, 0, pl.ds(cown + half, cown), :] = outer[cown:]
        outer = jnp.concatenate(
            [row_pairs(side, c, 0, first, cown) for first in (0, own + size)], axis=0
        )
        outer = dot(outer, edge)
        fill_coarse(c, -cown, outer[:cown])
        fill_coarse(c, half, outer[cown:])
    for first in (own - 11, own + size - 4):
        bed_slopes(state, slopes, first, 16, 16, 2)
        bed_slopes(side, sslopes, first, 16, 16, 1)
    for first in (own + half // 2 - 5, own + half // 2 + half - 3):
        bed_slopes(side, sslopes, first, 8, 8, 1)
    for first in (cown - 5, cown + half - 3):
        bed_slopes(cstate, cslopes, first, 8, 8, 1)
    for k in range(6):
        gone = 2 * (k + 1)
        wide = 12 - gone
        blocks = [(own - wide - 3, 16), (own + size - gone + 1, 16)]
        all_three = [fine_stage(k, blocks)]
        if k < 3:
            cblocks = [(cown - 6 + gone - 3, 16), (cown + half - gone + 1, 8)]
            all_three.append(coarse_stage(k, cblocks))
            blocks = blocks + [(r + own + half // 2 - cown, rows) for r, rows in cblocks]
        all_three.append(side_stage(k, blocks))
        together(*all_three)

    errors = []
    lane = lane_ids((half, L))
    for c in range(3):
        edges = row_pairs(sbufs.at[5], c, 0, own, half)
        both = [row_pairs(bufs.at[5], c, t, own, half) for t in range(2)]
        both = [
            jnp.where(lane < 12, pltpu.roll(edges, L - 32, axis=1), both[0]),
            jnp.where(lane >= L - 12, edges, both[1]),
        ]
        edges = sbufs[2, c, 0, pl.ds(own + half // 2, half), :]
        rough = cbufs[2, c, 0, pl.ds(cown, half), :]
        rough = jnp.where(lane >= L - 6, pltpu.roll(edges, 60, axis=1), rough)
        rough = jnp.where(lane < 6, pltpu.roll(edges, L - 84, axis=1), rough)
        back = ERROR_SCALE / (HELD_M if c else HELD_H)
        errors.append(jnp.abs(dot(jnp.concatenate(both, axis=1), pairs) - rough) * back)
        e_held[c] = errors[c]
    error = jnp.concatenate(errors, axis=0)
    for c in range(3):
        sums = dot(x_weight, errors[c]) * x_keep
        for d in range(nr):
            xs[d, pl.ds(c * per_row, per_row), :] = sums[d * per_row : (d + 1) * per_row]
    copies = []
    for d in sorted(range(1, nr), key=lambda d: -abs(2 * d - nr)):
        other = lax.rem(row + d, nr)
        copies.append(
            pltpu.make_async_remote_copy(
                src_ref=xs.at[other, pl.ds(0, 3 * per_row)],
                dst_ref=xr.at[row, pl.ds(0, 3 * per_row)],
                send_sem=xs_sem.at[d],
                recv_sem=xr_sem.at[d],
                device_id=(other, col),
                device_id_type=MESH,
            )
        )
        copies[-1].start()
    summed = lax.dot_general(
        y_weight, error, (((1,), (1,)), ((), ())), precision=HIGHEST,
        preferred_element_type=jnp.float32,
    )
    ys[:, pl.ds(0, 3 * half)] = summed * y_keep
    for d in range(1, nc):
        other = lax.rem(col + d, nc)
        copies.append(
            pltpu.make_async_remote_copy(
                src_ref=ys.at[pl.ds(pl.multiple_of(other * per_col, 8), per_col), :],
                dst_ref=yr.at[col],
                send_sem=ys_sem.at[d],
                recv_sem=yr_sem.at[d],
                device_id=(row, other),
                device_id_type=MESH,
            )
        )
        copies[-1].start()
    e_copy = pltpu.make_async_copy(e_held, e_ref, load_sem.at[0])
    e_copy.start()
    xr[row] = xs[row]
    yr[col] = ys[pl.ds(pl.multiple_of(col * per_col, 8), per_col), :]
    for copy in copies:
        copy.wait()
    e_copy.wait()
    x_sum = xr[0]
    for d in range(1, nr):
        x_sum = x_sum + xr[d]
    for c in range(3):
        x_ref[c] = x_sum[c * per_row : (c + 1) * per_row]
    y_sum = yr[0]
    for d in range(1, nc):
        y_sum = y_sum + yr[d]
    for c in range(3):
        y_ref[c] = y_sum[:, c * half : (c + 1) * half]


def write_out(e, x, y, e_out, x_out, y_out, sems):
    pairs = ((e, e_out), (x, x_out), (y, y_out))
    copies = [pltpu.make_async_copy(a, b, sems.at[i]) for i, (a, b) in enumerate(pairs)]
    for copy in copies:
        copy.start()
    for copy in copies:
        copy.wait()


def on_device(nr, nc, depth, momentum_x, momentum_y, bathymetry, boxes):
    size = depth.shape[0]
    half = size // 2
    number = boxes.shape[0]
    pad = -(-4 * (number // nr) // 8) * 8
    rows = size + 2 * HALO + 32
    crows = half + HALO + 32
    f32 = jnp.float32
    vmem = pltpu.VMEM
    sems = pltpu.SemaphoreType.DMA
    halo_copies = 5 if nc == 2 else 8
    hbm = pl.BlockSpec(memory_space=pltpu.HBM)
    inside = pl.BlockSpec(memory_space=pltpu.VMEM)
    shapes = (
        jax.ShapeDtypeStruct((3, half, L), f32),
        jax.ShapeDtypeStruct((3, number // nr, L), f32),
        jax.ShapeDtypeStruct((3, number // nc, half), f32),
    )
    results = pl.pallas_call(
        functools.partial(kernel, nr, nc),
        out_shape=shapes,
        in_specs=[hbm] * 5,
        out_specs=(hbm, inside, inside),
        scratch_shapes=[
            vmem((4, 2, size, L), f32),
            vmem((4, 2, rows, L), f32),
            vmem((6, 3, 2, rows, L), f32),
            vmem((4, 3, 2, rows, L), f32),
            vmem((2, 2, rows, L), f32),
            vmem((6, 3, 2, rows, L), f32),
            vmem((6, 3, 2, rows, L), f32),
            vmem((6, 3, 2, rows, L), f32),
            vmem((size, L), f32),
            vmem((1 if nc == 2 else 2, size + 2 * HALO, L), f32),
            vmem((2, 4, 2, HALO, L), f32),
            vmem((4, 1, rows, L), f32),
            vmem((6, 3, 1, rows, L), f32),
            vmem((4, 3, 1, rows, L), f32),
            vmem((2, 1, rows, L), f32),
            vmem((6, 3, 1, rows, L), f32),
            vmem((6, 3, 1, rows, L), f32),
            vmem((6, 3, 1, rows, L), f32),
            vmem((4, 1, crows, L), f32),
            vmem((3, 3, 1, crows, L), f32),
            vmem((2, 3, 1, crows, L), f32),
            vmem((2, 1, crows, L), f32),
            vmem((3, 3, 1, crows, L), f32),
            vmem((3, 3, 1, crows, L), f32),
            vmem((3, 3, 1, crows, L), f32),
            vmem((nr, pad, L), f32),
            vmem((nr, pad, L), f32),
            vmem((number, L), f32),
            vmem((nc, number // nc, L), f32),
            vmem((4, number), jnp.int32),
            vmem((3, half, L), f32),
            sems((9,)),
            sems((halo_copies,)),
            sems((halo_copies,)),
            sems((nr,)),
            sems((nr,)),
            sems((nc,)),
            sems((nc,)),
        ],
        compiler_params=pltpu.CompilerParams(
            collective_id=0, has_side_effects=True, vmem_limit_bytes=63 * 1024 * 1024
        ),
    )(depth, momentum_x, momentum_y, bathymetry, boxes.T)
    error, x_sig, y_sig = pl.pallas_call(
        write_out,
        out_shape=shapes,
        in_specs=[inside] * 3,
        out_specs=(hbm,) * 3,
        scratch_shapes=[sems((3,))],
    )(*results)
    return error, jnp.transpose(x_sig, (1, 0, 2)), jnp.transpose(y_sig, (1, 0, 2))


def solution(mesh):
    placed = (P("row", "col"), P("row", "col"), P("row", "col"), P("row", "col"), P())
    return jax.shard_map(
        functools.partial(on_device, mesh.shape["row"], mesh.shape["col"]),
        mesh=mesh,
        in_specs=placed,
        out_specs=(P(None, "row", "col"), P("row", None, "col"), P("col", None, "row")),
        check_vma=False,
    )
```
